256 devices in a mesh: row: 8 (over y, core), col: 8 (over x, z_hi), rep: 4 (over z_lo).
Axes of the slice: x: 4, y: 4, z: 8 (z_hi: 2, z_lo: 4; z = z_hi * 4 + z_lo), core: 2. Of those that a mesh axis runs over, the one named last changes fastest.
Arguments:
- features: float32 [256, 32768], P('rep', ('col', 'row')), may hold values from -6 to 6
- weight: float32 [256, 256], replicated, may hold values from -0.375 to 0.375
- cotangent: float32 [256, 32768], P('rep', ('row', 'col')), may hold values from -6 to 6
- tile_values: float32 [10240, 128, 128], P(('row', 'col')), may hold values from -0.078125 to 0.078125
- tile_row: int32 [10240], P(('row', 'col')), may hold values from 0 to 31
- tile_col: int32 [10240], P(('row', 'col')), may hold values from 0 to 31
- tile_kind: int32 [10240], P(('row', 'col')), may hold values from 0 to 159
- tile_count: int32 [64], P(('row', 'col')), may hold values from 40 to 160, as said below
Outputs:
- output: float32 [256, 32768], P('rep', ('row', 'col'))
- input_grad: float32 [256, 32768], P('rep', ('col', 'row'))
- weight_grad: float32 [256, 256], P('rep')
The draws below stay inside these ranges and needn't reach their ends.
Inputs may be any that keep to these rules, and one draw needn't show every extreme that they name: `tile_count`: a block's slots at or after its count are not part of the adjacency; some block uses all 160 slots. `tile_row`: slots may repeat a tile position; their tiles add. `tile_kind`: an index into the 160 stored tiles of the same block.
All inputs are finite; a program needn't handle non-finite values.
Results may differ from the reference program's by a relative error of at most 0.0001.
Values sent between devices are 32-bit elements; how exact they have to be, the bound alone decides.
No kernel may reach another device: no remote copies, remote signals or barrier semaphores. Data moves between devices by JAX's collectives and lax.ppermute only.
A program may use at most 128 MiB of HBM per device.

```python
import jax
import jax.numpy as jnp
from jax import lax

F = 256
TILE = 128
CT = 4
TD = 160
BLOCKS = 64
NODES = 32768
N_ROW = 8
N_COL = 8


def draw_tile_count(key, part):
    lowest = max(TD // 4, 1)
    counts = jax.random.randint(key, (BLOCKS,), lowest, TD + 1)
    fullest = jax.random.randint(jax.random.fold_in(key, 7), (), 0, BLOCKS)
    return jnp.where(jnp.arange(BLOCKS) == fullest, TD, counts).astype(jnp.int32)


def place_ends(drawn, own_key, least, largest):
    longest = drawn.shape.index(max(drawn.shape))
    spots = []
    for shift in (0, 1):
        where = [jax.random.randint(jax.random.fold_in(own_key, axis), (), 0, length) for axis, length in enumerate(drawn.shape)]
        where[longest] = (where[longest] + shift) % drawn.shape[longest]
        spots.append(tuple(where))
    return drawn.at[spots[0]].set(least).at[spots[1]].set(largest)


def block_scale(key, shape, cuts, low, high):
    loudness, own = 1.0, jax.random.fold_in(key, 6)
    for position, parts in cuts:
        steps = jnp.exp(jax.random.uniform(jax.random.fold_in(own, position), (parts,), jnp.float32, low / len(cuts), high / len(cuts)))
        loudness = loudness * jnp.repeat(steps, shape[position] // parts).reshape([-1 if axis == position else 1 for axis in range(len(shape))])
    return loudness


def bell_draw(own_key, extent, width, reach, shards=(), kind=jnp.bfloat16):
    level = block_scale(own_key, extent, shards, -0.22, 0.18) if shards else 1.0
    drawn = jax.random.normal(own_key, extent, jnp.float32) * width * level
    return jnp.minimum(jnp.maximum(drawn, -reach), reach).astype(kind)


def setup_inputs(seed: int = 0) -> dict:
    streams_of = jax.random.split(jax.random.key(seed), 9)
    features = bell_draw(streams_of[0], (F, NODES), 1.0, 6.0, ((0, 4), (1, 64)), jnp.float32)
    weight = bell_draw(streams_of[1], (F, F), F ** -0.5, 0.375, (), jnp.float32)
    cotangent = bell_draw(streams_of[2], (F, NODES), 1.0, 6.0, ((0, 4), (1, 64)), jnp.float32)
    tile_values = bell_draw(streams_of[3], (BLOCKS * TD, TILE, TILE), (TD * TILE // CT) ** -0.5, 0.078125, ((0, 64),), jnp.float32)
    tile_row = place_ends(jax.random.randint(streams_of[4], (BLOCKS * TD,), 0, N_COL * CT), jax.random.fold_in(streams_of[4], 1), 0, (N_COL * CT) - 1).astype(jnp.int32)
    tile_col = place_ends(jax.random.randint(streams_of[5], (BLOCKS * TD,), 0, N_ROW * CT), jax.random.fold_in(streams_of[5], 1), 0, (N_ROW * CT) - 1).astype(jnp.int32)
    tile_kind = place_ends(jax.random.randint(streams_of[6], (BLOCKS * TD,), 0, TD), jax.random.fold_in(streams_of[6], 1), 0, TD - 1).astype(jnp.int32)
    tile_count = draw_tile_count(jax.random.fold_in(streams_of[8], 71), 0)
    return dict(features=features, weight=weight, cotangent=cotangent, tile_values=tile_values, tile_row=tile_row, tile_col=tile_col, tile_kind=tile_kind, tile_count=tile_count)


def tile_terms(source, values, from_tile, to_tile, tile_kinds, live_weight, dest_tiles, transposed):
    feat_width = source.shape[0]
    tile_edge = values.shape[1]
    tiled = source.reshape(feat_width, source.shape[1] // tile_edge, tile_edge)
    picked = jnp.take(tiled, from_tile, axis=1)
    chosen = jnp.take(values, tile_kinds, axis=0)
    if transposed:
        products = jnp.einsum('fga,gab->fgb', picked, chosen, precision=lax.Precision.HIGHEST)
    else:
        products = jnp.einsum('fgb,gab->fga', picked, chosen, precision=lax.Precision.HIGHEST)
    onehot = (to_tile[:, None] == jnp.arange(dest_tiles, dtype=jnp.int32)[None, :]).astype(jnp.float32)
    onehot = onehot * live_weight[:, None]
    spread = jnp.einsum('fgt,gd->fdt', products, onehot, precision=lax.Precision.HIGHEST)
    return spread.reshape(feat_width, dest_tiles * tile_edge)

def reference(features, weight, cotangent, tile_values, tile_row, tile_col, tile_kind, tile_count):
    stretch_len = CT * TILE
    row_span = N_COL * stretch_len
    col_span = N_ROW * stretch_len
    mixed = jnp.dot(weight.T, features, preferred_element_type=jnp.float32, precision=lax.Precision.HIGHEST)
    pre = jnp.zeros_like(mixed)
    slot_ids = jnp.arange(TD, dtype=jnp.int32)
    for row_block in range(N_ROW):
        for col_block in range(N_COL):
            block_id = row_block * N_COL + col_block
            lower = block_id * TD
            live_weight = (slot_ids < tile_count[block_id]).astype(jnp.float32)
            values = tile_values[lower:lower + TD]
            source = mixed[:, col_block * col_span:(col_block + 1) * col_span]
            terms = tile_terms(source, values, tile_col[lower:lower + TD], tile_row[lower:lower + TD], tile_kind[lower:lower + TD], live_weight, N_COL * CT, False)
            pre = pre.at[:, row_block * row_span:(row_block + 1) * row_span].add(terms)
    output, pullback = jax.vjp(lambda v: jax.nn.gelu(v, approximate=True), pre)
    grad_pre, = pullback(cotangent)
    grad_mixed = jnp.zeros_like(mixed)
    for row_block in range(N_ROW):
        for col_block in range(N_COL):
            block_id = row_block * N_COL + col_block
            lower = block_id * TD
            live_weight = (slot_ids < tile_count[block_id]).astype(jnp.float32)
            values = tile_values[lower:lower + TD]
            source = grad_pre[:, row_block * row_span:(row_block + 1) * row_span]
            terms = tile_terms(source, values, tile_row[lower:lower + TD], tile_col[lower:lower + TD], tile_kind[lower:lower + TD], live_weight, N_ROW * CT, True)
            grad_mixed = grad_mixed.at[:, col_block * col_span:(col_block + 1) * col_span].add(terms)
    input_grad = jnp.dot(weight, grad_mixed, preferred_element_type=jnp.float32, precision=lax.Precision.HIGHEST)
    weight_grad = jnp.dot(features, grad_mixed.T, preferred_element_type=jnp.float32, precision=lax.Precision.HIGHEST)
    weight_grad = weight_grad * float(NODES) ** (-0.5)
    return (output, input_grad, weight_grad)
```

```python
import functools

import jax
import jax.numpy as jnp
from jax import lax
from jax.experimental import pallas as pl
from jax.experimental.pallas import tpu as pltpu
from jax.sharding import PartitionSpec as P


BF16 = jnp.bfloat16
F32 = jnp.float32
NT = (((1,), (1,)), ((), ()))
NN = (((1,), (0,)), ((), ()))
GROUP = 16
RING = 4
ROOT_2_PI = 0.7978845608028654
CUBIC = 0.044715

dot = functools.partial(lax.dot_general, preferred_element_type=F32)


def split(x):
    high = x.astype(BF16)
    return high, (x - high.astype(F32)).astype(BF16)


def dot3(a, b, dims):
    a_high, a_low = split(a)
    b_high, b_low = split(b)
    return dot(a_high, b_high, dims) + dot(a_high, b_low, dims) + dot(a_low, b_high, dims)


def prep_kernel(kinds, values_ref, tiles_ref, buf, sem):
    step = pl.program_id(0)
    steps = pl.num_programs(0)

    def copy(group, u):
        slot = lax.rem(group, 2)
        return pltpu.make_async_copy(
            values_ref.at[kinds[group * GROUP + u]], buf.at[slot, u], sem.at[slot, u]
        )

    @pl.when(step == 0)
    def _():
        for u in range(GROUP):
            copy(step, u).start()

    @pl.when(step + 1 < steps)
    def _():
        for u in range(GROUP):
            copy(step + 1, u).start()

    slot = lax.rem(step, 2)
    for u in range(GROUP):
        copy(step, u).wait()
        high, low = split(buf[slot, u])
        tiles_ref[u, 0] = high
        tiles_ref[u, 1] = low


def prep(kinds, values):
    slots, edge, _ = values.shape
    return pl.pallas_call(
        prep_kernel,
        grid_spec=pltpu.PrefetchScalarGridSpec(
            num_scalar_prefetch=1,
            grid=(slots // GROUP,),
            in_specs=[pl.BlockSpec(memory_space=pl.ANY)],
            out_specs=pl.BlockSpec((GROUP, 2, edge, edge), lambda g, kinds: (g, 0, 0, 0)),
            scratch_shapes=[
                pltpu.VMEM((2, GROUP, edge, edge), F32),
                pltpu.SemaphoreType.DMA((2, GROUP)),
            ],
        ),
        out_shape=jax.ShapeDtypeStruct((slots, 2, edge, edge), BF16),
        compiler_params=pltpu.CompilerParams(vmem_limit_bytes=52 << 20),
        cost_estimate=pl.CostEstimate(flops=0, bytes_accessed=24 << 20, transcendentals=0),
        name="prep",
    )(kinds, values)


def spmm_kernel(transposed, n_in, n_out, table, *refs):
    sources = refs[:n_in]
    tiles = refs[n_in]
    outs = refs[n_in + 1 : n_in + 1 + n_out]
    buf, sem, held, acc = refs[n_in + 1 + n_out :]
    width, length = sources[0].shape
    edge = tiles.shape[-1]
    per = length // edge
    to_row, from_row = (2, 3) if transposed else (0, 1)
    groups = (table[4, 0] + GROUP - 1) // GROUP

    def copy(group):
        slot = lax.rem(group, RING)
        return pltpu.make_async_copy(
            tiles.at[pl.ds(group * GROUP, GROUP)], buf.at[slot], sem.at[slot]
        )

    for g in range(RING - 1):

        @pl.when(g < groups)
        def _():
            copy(g).start()

    for b in range(n_in):
        for j in range(per):
            high, low = split(sources[b][:, j * edge : (j + 1) * edge])
            held[b * per + j, :width] = high
            held[b * per + j, width:] = low
    acc[...] = jnp.zeros_like(acc)

    def step(group, carry):
        @pl.when(group + RING - 1 < groups)
        def _():
            copy(group + RING - 1).start()

        copy(group).wait()
        slot = lax.rem(group, RING)
        products = []
        for u in range(GROUP):
            both = held[table[from_row, group * GROUP + u]]
            if transposed:
                p = dot(both, buf[slot, u, 0], NN)
                products.append(p[:width] + p[width:] + dot(both[:width], buf[slot, u, 1], NN))
            else:
                p = dot(both, buf[slot, u].reshape(2 * edge, edge), NT)
                products.append(p[:width, :edge] + p[:width, edge:] + p[width:, :edge])
        for u in range(GROUP):
            to = table[to_row, group * GROUP + u]
            acc[to] = acc[to] + products[u]
        return carry

    lax.fori_loop(0, groups, step, 0)
    for b in range(n_out):
        for j in range(per):
            outs[b][:, j * edge : (j + 1) * edge] = acc[b * per + j]


def spmm(table, sources, tiles, n_out, transposed):
    n_in = len(sources)
    width, length = sources[0].shape
    slots, _, edge, _ = tiles.shape
    per = length // edge
    vmem = pl.BlockSpec(memory_space=pltpu.VMEM)
    return pl.pallas_call(
        functools.partial(spmm_kernel, transposed, n_in, n_out),
        in_specs=[pl.BlockSpec(memory_space=pltpu.SMEM)]
        + [vmem] * n_in
        + [pl.BlockSpec(memory_space=pl.ANY)],
        out_specs=[vmem] * n_out,
        out_shape=[jax.ShapeDtypeStruct((width, length), F32)] * n_out,
        scratch_shapes=[
            pltpu.VMEM((RING, GROUP, 2, edge, edge), BF16),
            pltpu.SemaphoreType.DMA((RING,)),
            pltpu.VMEM((n_in * per, 2 * width, edge), BF16),
            pltpu.VMEM((n_out * per + 1, width, edge), F32),
        ],
        compiler_params=pltpu.CompilerParams(vmem_limit_bytes=52 << 20),
        cost_estimate=pl.CostEstimate(
            flops=6 * slots * width * edge * edge, bytes_accessed=14 << 20, transcendentals=0
        ),
        name="spmm_back" if transposed else "spmm",
    )(table, *sources, tiles)


def mid_kernel(n_rep, place, *refs):
    aggs = refs[:n_rep]
    cots = refs[n_rep : 2 * n_rep]
    weight, weight_t, out, mixed_grad, grad_pre = refs[2 * n_rep : 2 * n_rep + 5]
    agg, cot, act = refs[2 * n_rep + 5 :]
    quarter = aggs[0].shape[0]
    me = place[0]
    for k in range(n_rep):
        at = pl.ds(pl.multiple_of((me ^ k) * quarter, quarter), quarter)
        agg[at, :] = aggs[k][...]
        cot[at, :] = cots[k][...]
    pre = dot3(weight_t[...], agg[...], NN)
    square = pre * pre
    curve = jnp.tanh(ROOT_2_PI * (pre + CUBIC * (square * pre)))
    half = 0.5 * (1.0 + curve)
    act[...] = pre * half
    slope = half + 0.5 * pre * (1.0 - curve * curve) * (
        ROOT_2_PI * (1.0 + 3.0 * CUBIC * square)
    )
    grad = cot[...] * slope
    grad_pre[...] = grad
    own = pl.ds(pl.multiple_of(me * quarter, quarter), quarter)
    mixed_grad[...] = dot3(weight[own, :], grad, NN)
    out[...] = act[own, :]


def mid(place, aggs, cots, weight, weight_t):
    n_rep = len(aggs)
    quarter, length = aggs[0].shape
    width = weight.shape[0]
    vmem = pl.BlockSpec(memory_space=pltpu.VMEM)
    return pl.pallas_call(
        functools.partial(mid_kernel, n_rep),
        in_specs=[pl.BlockSpec(memory_space=pltpu.SMEM)] + [vmem] * (2 * n_rep + 2),
        out_specs=[vmem] * 3,
        out_shape=[
            jax.ShapeDtypeStruct((quarter, length), F32),
            jax.ShapeDtypeStruct((quarter, length), F32),
            jax.ShapeDtypeStruct((width, length), F32),
        ],
        scratch_shapes=[pltpu.VMEM((width, length), F32)] * 3,
        compiler_params=pltpu.CompilerParams(vmem_limit_bytes=16 << 20),
        cost_estimate=pl.CostEstimate(
            flops=8 * width * width * length, bytes_accessed=4 << 20, transcendentals=0
        ),
        name="mid",
    )(place, *aggs, *cots, weight, weight_t)


def weight_kernel(scale, agg, grad_pre, out):
    out[...] = dot3(agg[...], grad_pre[...], NT) * scale


def weight_part(agg, grad_pre, scale):
    vmem = pl.BlockSpec(memory_space=pltpu.VMEM)
    return pl.pallas_call(
        functools.partial(weight_kernel, scale),
        in_specs=[vmem, vmem],
        out_specs=vmem,
        out_shape=jax.ShapeDtypeStruct((agg.shape[0], grad_pre.shape[0]), F32),
        compiler_params=pltpu.CompilerParams(vmem_limit_bytes=16 << 20),
        cost_estimate=pl.CostEstimate(
            flops=6 * agg.shape[0] * grad_pre.size, bytes_accessed=1 << 20, transcendentals=0
        ),
        name="weight_part",
    )(agg, grad_pre)


def shift(x, axis, by):
    n = lax.axis_size(axis)
    return lax.ppermute(x, axis, [(i, (i + by) % n) for i in range(n)])


def swap(x, axis, bit):
    n = lax.axis_size(axis)
    return lax.ppermute(x, axis, [(i, i ^ bit) for i in range(n)])


def local(features, weight, cotangent, tile_values, tile_row, tile_col, tile_kind, tile_count):
    n_row, n_col, n_rep = (lax.axis_size(a) for a in ("row", "col", "rep"))
    row, col, rep = (lax.axis_index(a) for a in ("row", "col", "rep"))
    stretch = features.shape[1]
    per = stretch // tile_values.shape[1]
    slots = tile_kind.shape[0]

    def relative(tile, at, n):
        stretch_of = tile // per
        far = (stretch_of // 2 - at // 2) % (n // 2)
        return (far * 2 + ((stretch_of ^ at) & 1)) * per + tile % per

    live = jnp.arange(slots, dtype=jnp.int32) < tile_count[0]
    by_row = relative(tile_row, col, n_col)
    by_col = relative(tile_col, row, n_row)
    table = jnp.stack(
        [
            jnp.where(live, by_row, n_col * per),
            by_col,
            jnp.where(live, by_col, n_row * per),
            by_row,
            jnp.broadcast_to(tile_count, (slots,)),
        ]
    )
    blocks = []
    for k in range(n_row // 2):
        mine = features if k == 0 else shift(features, "row", -2 * k)
        blocks += [mine, swap(mine, "row", 1)]
    cots = [cotangent] + [swap(cotangent, "rep", k) for k in range(1, n_rep)]
    tiles = prep(tile_kind, tile_values)
    parts = spmm(table, blocks, tiles, n_col, False)
    sums = [None, None]
    for z in (1, 0):
        total = parts[z]
        for k in range(1, n_col // 2):
            total = total + shift(parts[2 * k + z], "col", 2 * k)
        sums[z] = total
    agg = sums[0] + swap(sums[1], "col", 1)
    aggs = [agg] + [swap(agg, "rep", k) for k in range(1, n_rep)]
    place = rep.astype(jnp.int32)[None]
    output, mixed_grad, grad_pre = mid(place, aggs, cots, weight, weight.T)
    far = swap(mixed_grad, "col", 1)
    blocks = [mixed_grad, far]
    for k in range(1, n_col // 2):
        blocks += [shift(mixed_grad, "col", -2 * k), shift(far, "col", -2 * k)]
    node_total = stretch * n_row * n_col
    weight_grad = weight_part(agg, grad_pre, float(node_total) ** (-0.5))
    for axis, bit in (("row", 1), ("row", 2), ("row", 4), ("col", 1), ("col", 2), ("col", 4)):
        weight_grad = weight_grad + swap(weight_grad, axis, bit)
    parts = spmm(table, blocks, tiles, n_row, True)
    input_grad = None
    for k in (2, 1, 3, 0):
        total = parts[2 * k] + swap(parts[2 * k + 1], "row", 1)
        if k:
            total = shift(total, "row", 2 * k)
        input_grad = total if input_grad is None else input_grad + total
    return (output, input_grad, weight_grad)


def solution(mesh):
    return jax.shard_map(
        local,
        mesh=mesh,
        in_specs=(
            P("rep", ("col", "row")),
            P(),
            P("rep", ("row", "col")),
            P(("row", "col"), None, None),
            P(("row", "col")),
            P(("row", "col")),
            P(("row", "col")),
            P(("row", "col")),
        ),
        out_specs=(P("rep", ("row", "col")), P("rep", ("col", "row")), P("rep", None)),
        check_vma=False,
    )
```

```python
import functools
import math

import jax
import jax.numpy as jnp
from jax import lax
from jax.experimental import pallas as pl
from jax.experimental.pallas import tpu as pltpu
from jax.sharding import PartitionSpec as P


BF16 = jnp.bfloat16
F32 = jnp.float32
NT = (((1,), (1,)), ((), ()))
NN = (((1,), (0,)), ((), ()))
GROUP = 16
RING = 4
ROOT_2_PI = 0.7978845608028654
CUBIC = 0.044715
BIG = 51 << 20
SMALL = 16 << 20

dot = functools.partial(lax.dot_general, preferred_element_type=F32)


def split(x):
    high = x.astype(BF16)
    return high, (x - high.astype(F32)).astype(BF16)


def dot3(a, b, dims):
    a_high, a_low = split(a)
    b_high, b_low = split(b)
    return dot(a_high, b_high, dims) + dot(a_high, b_low, dims) + dot(a_low, b_high, dims)


def prep_kernel(first, kinds, values_ref, *refs):
    tiles_ref, buf, sem = refs[-3:]
    step = pl.program_id(0)
    steps = pl.num_programs(0)

    def copy(group, u):
        slot = lax.rem(group, 2)
        return pltpu.make_async_copy(
            values_ref.at[kinds[(first + group) * GROUP + u]], buf.at[slot, u], sem.at[slot, u]
        )

    def start(group):
        def one(u, carry):
            copy(group, u).start()
            return carry

        lax.fori_loop(0, GROUP, one, 0)

    @pl.when(step == 0)
    def _():
        start(step)

    @pl.when(step + 1 < steps)
    def _():
        start(step + 1)

    slot = lax.rem(step, 2)

    def convert(u, carry):
        copy(step, u).wait()
        high, low = split(buf[slot, u])
        tiles_ref[u, 0] = high
        tiles_ref[u, 1] = low
        return carry

    lax.fori_loop(0, GROUP, convert, 0)


def prep(kinds, values, first, count, into=None):
    slots, edge, _ = values.shape
    more = [] if into is None else [into]
    return pl.pallas_call(
        functools.partial(prep_kernel, first),
        grid_spec=pltpu.PrefetchScalarGridSpec(
            num_scalar_prefetch=1,
            grid=(count,),
            in_specs=[pl.BlockSpec(memory_space=pl.ANY)] * (1 + len(more)),
            out_specs=pl.BlockSpec(
                (GROUP, 2, edge, edge), lambda g, kinds: (first + g, 0, 0, 0)
            ),
            scratch_shapes=[
                pltpu.VMEM((2, GROUP, edge, edge), F32),
                pltpu.SemaphoreType.DMA((2, GROUP)),
            ],
        ),
        out_shape=jax.ShapeDtypeStruct((slots, 2, edge, edge), BF16),
        input_output_aliases={2: 0} if more else {},
        compiler_params=pltpu.CompilerParams(vmem_limit_bytes=BIG),
        cost_estimate=pl.CostEstimate(flops=0, bytes_accessed=12 << 20, transcendentals=0),
        name="prep",
    )(kinds, values, *more)


def spmm_kernel(transposed, n_in, n_out, table, *refs):
    sources = refs[:n_in]
    tiles = refs[n_in]
    outs = refs[n_in + 1 : n_in + 1 + n_out]
    buf, sem, held, acc = refs[n_in + 1 + n_out :]
    edge = tiles.shape[-1]
    width = acc.shape[1]
    to_row, from_row = (2, 3) if transposed else (0, 1)
    groups = (table[4, 0] + GROUP - 1) // GROUP

    def copy(group):
        slot = lax.rem(group, RING)
        return pltpu.make_async_copy(
            tiles.at[pl.ds(group * GROUP, GROUP)], buf.at[slot], sem.at[slot]
        )

    for g in range(RING - 1):

        @pl.when(g < groups)
        def _():
            copy(g).start()

    at = 0
    for ref in sources:
        for j in range(ref.shape[-1] // edge if ref.ndim == 2 else ref.shape[0]):
            high, low = split(ref[:, j * edge : (j + 1) * edge] if ref.ndim == 2 else ref[j])
            held[at, :width] = high
            held[at, width:] = low
            at += 1
    acc[...] = jnp.zeros_like(acc)

    def step(group, carry):
        @pl.when(group + RING - 1 < groups)
        def _():
            copy(group + RING - 1).start()

        copy(group).wait()
        slot = lax.rem(group, RING)
        products = []
        for u in range(GROUP):
            both = held[table[from_row, group * GROUP + u]]
            if transposed:
                p = dot(both, buf[slot, u, 0], NN)
                products.append(p[:width] + p[width:] + dot(both[:width], buf[slot, u, 1], NN))
            else:
                p = dot(both, buf[slot, u].reshape(2 * edge, edge), NT)
                products.append(p[:width, :edge] + p[:width, edge:] + p[width:, :edge])
        for u in range(GROUP):
            to = table[to_row, group * GROUP + u]
            acc[to] = acc[to] + products[u]
        return carry

    lax.fori_loop(0, groups, step, 0)
    at = 0
    for ref in outs:
        if ref.ndim == 3:
            ref[...] = acc[at : at + ref.shape[0]]
            at += ref.shape[0]
        else:
            for j in range(ref.shape[-1] // edge):
                ref[:, j * edge : (j + 1) * edge] = acc[at]
                at += 1


def spmm(table, sources, tiles, out_shape, n_out, width, transposed):
    n_in = len(sources)
    slots, _, edge, _ = tiles.shape
    n_from = sum(x.size for x in sources) // (width * edge)
    n_to = n_out * math.prod(out_shape) // (width * edge)
    vmem = pl.BlockSpec(memory_space=pltpu.VMEM)
    return pl.pallas_call(
        functools.partial(spmm_kernel, transposed, n_in, n_out),
        in_specs=[pl.BlockSpec(memory_space=pltpu.SMEM)]
        + [vmem] * n_in
        + [pl.BlockSpec(memory_space=pl.ANY)],
        out_specs=[vmem] * n_out,
        out_shape=[jax.ShapeDtypeStruct(out_shape, F32)] * n_out,
        scratch_shapes=[
            pltpu.VMEM((RING, GROUP, 2, edge, edge), BF16),
            pltpu.SemaphoreType.DMA((RING,)),
            pltpu.VMEM((n_from, 2 * width, edge), BF16),
            pltpu.VMEM((n_to + 1, width, edge), F32),
        ],
        compiler_params=pltpu.CompilerParams(vmem_limit_bytes=BIG),
        cost_estimate=pl.CostEstimate(
            flops=6 * slots * width * edge * edge, bytes_accessed=14 << 20, transcendentals=0
        ),
        name="spmm_back" if transposed else "spmm",
    )(table, *sources, tiles)


def small(body, out_shapes, *args, scalars=1, scratch=(), flops=1 << 20, name=None):
    vmem = pl.BlockSpec(memory_space=pltpu.VMEM)
    call = pl.pallas_call(
        body,
        in_specs=[pl.BlockSpec(memory_space=pltpu.SMEM)] * scalars
        + [vmem] * (len(args) - scalars),
        out_specs=[vmem] * len(out_shapes),
        out_shape=[jax.ShapeDtypeStruct(shape, F32) for shape in out_shapes],
        scratch_shapes=[pltpu.VMEM(shape, F32) for shape in scratch],
        compiler_params=pltpu.CompilerParams(vmem_limit_bytes=SMALL),
        cost_estimate=pl.CostEstimate(flops=flops, bytes_accessed=1 << 20, transcendentals=0),
        name=name,
    )
    return list(call(*args))


def part(n, size, index):
    return pl.ds(pl.multiple_of(lax.rem(index + 2 * n, n) * size, size), size)


def cut_kernel(place, whole, *outs):
    n = len(outs)
    size = whole.shape[1] // n
    for d in range(n):
        outs[d][...] = whole[:, part(n, size, place[0] + d)]


def join_kernel(place, *refs):
    out = refs[-1]
    n = len(refs) - 1
    size = out.shape[1] // n
    for d in range(n):
        out[:, part(n, size, place[0] - d)] = refs[d][...]


def fold_kernel(n, *refs):
    for i in range(refs[0].shape[0]):
        total = refs[0][i]
        for k in range(1, n):
            total = total + refs[k][i]
        refs[n + i][...] = total


def stack_kernel(*refs):
    for i in range(len(refs) - 1):
        refs[-1][i] = refs[i][...]


def mid_kernel(n_rep, n_z, place, *refs):
    sums = refs[:n_z]
    cots = refs[n_z : n_z + n_rep]
    weight, weight_t = refs[n_z + n_rep : n_z + n_rep + 2]
    refs = refs[n_z + n_rep + 2 :]
    grads = refs[:n_rep]
    acts = refs[n_rep : 2 * n_rep]
    agg, grad_pre, cot, act, mixed_grad = refs[2 * n_rep :]
    quarter = sums[0].shape[0]
    me = place[0]
    for d in range(n_rep):
        total = sums[d][...]
        for e in range(d + n_rep, n_z, n_rep):
            total = total + sums[e][...]
        agg[part(n_rep, quarter, me - d), :] = total
        cot[part(n_rep, quarter, me - d), :] = cots[d][...]
    pre = dot3(weight_t[...], agg[...], NN)
    square = pre * pre
    curve = jnp.tanh(ROOT_2_PI * (pre + CUBIC * (square * pre)))
    half = 0.5 * (1.0 + curve)
    act[...] = pre * half
    slope = half + 0.5 * pre * (1.0 - curve * curve) * (
        ROOT_2_PI * (1.0 + 3.0 * CUBIC * square)
    )
    grad = cot[...] * slope
    grad_pre[...] = grad
    mixed_grad[...] = dot3(weight[...], grad, NN)
    for d in range(n_rep):
        grads[d][...] = mixed_grad[part(n_rep, quarter, me + d), :]
        acts[d][...] = act[part(n_rep, quarter, me + d), :]


def weight_kernel(scale, place, agg, grad_pre, *refs):
    outs, total = refs[:-1], refs[-1]
    n = len(outs)
    total[...] = dot3(agg[...], grad_pre[...], NT) * scale
    for d in range(n):
        outs[d][...] = total[part(n, total.shape[0] // n, place[0] + d), :]


def shift(x, axis, by):
    n = lax.axis_size(axis)
    return lax.ppermute(x, axis, [(i, (i + by) % n) for i in range(n)])


def shift_z(x, by):
    n = lax.axis_size(("col", "rep"))
    m = 2 * lax.axis_size("rep")
    return lax.ppermute(x, ("col", "rep"), [(i, i // m * m + (i + by) % m) for i in range(n)])


def swap(x, axis, bit):
    n = lax.axis_size(axis)
    return lax.ppermute(x, axis, [(i, i ^ bit) for i in range(n)])


def local(features, weight, cotangent, tile_values, tile_row, tile_col, tile_kind, tile_count):
    n_row, n_col, n_rep = (lax.axis_size(a) for a in ("row", "col", "rep"))
    row, col, rep = (lax.axis_index(a) for a in ("row", "col", "rep"))
    n_x, n_y, n_z = n_col // 2, n_row // 2, 2 * n_rep
    width, stretch = features.shape
    edge = tile_values.shape[1]
    per = stretch // edge
    slots = tile_kind.shape[0]
    full = weight.shape[0]
    z = (col & 1) * n_rep + rep
    place = rep.astype(jnp.int32)[None]

    far_x = ((tile_row // n_z - col // 2) & (n_x - 1)) * n_z
    at_z = tile_row & (n_z - 1)
    stretch_of = tile_col // per
    far_y = (stretch_of // 2 - row // 2) & (n_y - 1)
    by_col = (far_y * 2 + ((stretch_of ^ row) & 1)) * per + (tile_col & (per - 1))
    live = jnp.arange(slots, dtype=jnp.int32) < tile_count[0]
    table = jnp.stack(
        [
            jnp.where(live, far_x + ((at_z - z - 2) & (n_z - 1)), n_x * n_z),
            by_col,
            jnp.where(live, by_col, n_row * per),
            far_x + ((z - at_z + 1) & (n_z - 1)),
            jnp.broadcast_to(tile_count, (slots,)),
        ]
    )
    mine = [features] + [shift(features, "row", -2 * k) for k in range(1, n_y)]
    half = slots // GROUP // 2
    tiles = prep(tile_kind, tile_values, 0, half)
    cots = small(cut_kernel, [(width, edge)] * n_rep, place, cotangent, name="cut")
    cots = cots[:1] + [shift(cots[d], "rep", d) for d in range(1, n_rep)]
    kinds, tiles, *mine[1:] = lax.optimization_barrier((tile_kind, tiles, *mine[1:]))
    blocks = []
    for x in mine:
        blocks += [x, swap(x, "row", 1)]
    tiles = prep(kinds, tile_values, half, slots // GROUP - half, tiles)
    table, *cots = lax.optimization_barrier((table, *cots))
    parts = spmm(table, blocks, tiles, (n_z // 2, width, edge), 2 * n_x, width, False)
    order = [(2 + i) % n_z for i in range(n_z)]
    sums = [None] * n_z
    for h in range(2):
        got = [parts[h]] + [shift(parts[2 * k + h], "col", 2 * k) for k in range(1, n_x)]
        folded = small(
            functools.partial(fold_kernel, n_x),
            [(width, edge)] * (n_z // 2), *got, scalars=0, name="fold",
        )
        for i in range(n_z // 2):
            d = order[h * n_z // 2 + i]
            sums[d] = shift_z(folded[i], d) if d else folded[i]
    *outs, agg, grad_pre = small(
        functools.partial(mid_kernel, n_rep, n_z),
        [(width, edge)] * (2 * n_rep) + [(full, edge)] * 2,
        place, *sums, *cots, weight, weight.T,
        scratch=[(full, edge)] * 3, flops=12 * full * full * edge, name="mid",
    )
    grads, acts = outs[:n_rep], outs[n_rep:]
    order = [(n_z - 1 + i) % n_z for i in range(n_z)]
    pieces = {d: shift_z(grads[d % n_rep], d) if d else grads[0] for d in range(n_z)}
    near = []
    for h in range(2):
        near += small(
            stack_kernel, [(n_z // 2, width, edge)],
            *[pieces[d] for d in order[h * n_z // 2 : (h + 1) * n_z // 2]],
            scalars=0, name="stack",
        )
    blocks = list(near)
    for k in range(1, n_x):
        blocks += [shift(x, "col", -2 * k) for x in near]
    acts = acts[:1] + [shift(acts[d], "rep", d) for d in range(1, n_rep)]
    (output,) = small(join_kernel, [(width, stretch)], place, *acts, name="join")
    scale = float(stretch * n_row * n_col) ** (-0.5)
    quarters = small(
        functools.partial(weight_kernel, scale),
        [(full // n_rep, full)] * n_rep, place, agg, grad_pre,
        scratch=[(full, full)], flops=6 * full * full * edge, name="weight_part",
    )
    weight_grad = quarters[0]
    for d in range(1, n_rep):
        weight_grad = weight_grad + shift(quarters[d], "rep", d)
    for axis, bit in (("col", 1), ("col", 2), ("col", 4), ("row", 1), ("row", 2), ("row", 4)):
        weight_grad = weight_grad + swap(weight_grad, axis, bit)
    parts = spmm(table, blocks, tiles, (width, stretch), n_row, width, True)
    input_grad = None
    for k in (2, 1, 3, 0):
        total = parts[2 * k] + swap(parts[2 * k + 1], "row", 1)
        if k:
            total = shift(total, "row", 2 * k)
        input_grad = total if input_grad is None else input_grad + total
    return (output, input_grad, weight_grad)


def solution(mesh):
    return jax.shard_map(
        local,
        mesh=mesh,
        in_specs=(
            P("rep", ("col", "row")),
            P(),
            P("rep", ("row", "col")),
            P(("row", "col"), None, None),
            P(("row", "col")),
            P(("row", "col")),
            P(("row", "col")),
            P(("row", "col")),
        ),
        out_specs=(P("rep", ("row", "col")), P("rep", ("col", "row")), P("rep", None)),
        check_vma=False,
    )
```

```python
import functools

import jax
import jax.numpy as jnp
from jax import lax
from jax.experimental import pallas as pl
from jax.experimental.pallas import tpu as pltpu
from jax.sharding import PartitionSpec as P


BF16 = jnp.bfloat16
F32 = jnp.float32
NT = (((1,), (1,)), ((), ()))
NN = (((1,), (0,)), ((), ()))
GROUP = 16
RING = 4
ROOT_2_PI = 0.7978845608028654
CUBIC = 0.044715

dot = functools.partial(lax.dot_general, preferred_element_type=F32)


def split(x):
    high = x.astype(BF16)
    return high, (x - high.astype(F32)).astype(BF16)


def dot3(a, b, dims):
    a_high, a_low = split(a)
    b_high, b_low = split(b)
    return dot(a_high, b_high, dims) + dot(a_high, b_low, dims) + dot(a_low, b_high, dims)


def spmm_kernel(transposed, n_in, n_out, table, *refs):
    sources = refs[:n_in]
    values = refs[n_in]
    outs = refs[n_in + 1 : n_in + 1 + n_out]
    buf, sem, held, acc = refs[n_in + 1 + n_out :]
    width, length = sources[0].shape
    edge = values.shape[-1]
    per = length // edge
    to_row, from_row = (2, 3) if transposed else (0, 1)
    groups = (table[5, 0] + GROUP - 1) // GROUP

    def copy(group, u):
        slot = lax.rem(group, RING)
        return pltpu.make_async_copy(
            values.at[table[4, group * GROUP + u]], buf.at[slot, u], sem.at[slot, u]
        )

    def start(group):
        def one(u, carry):
            copy(group, u).start()
            return carry

        lax.fori_loop(0, GROUP, one, 0, unroll=4)

    for g in range(RING - 1):

        @pl.when(g < groups)
        def _():
            start(g)

    for b in range(n_in):
        for j in range(per):
            high, low = split(sources[b][:, j * edge : (j + 1) * edge])
            held[b * per + j, :width] = high
            held[b * per + j, width:] = low
    acc[...] = jnp.zeros_like(acc)

    def step(group, carry):
        @pl.when(group + RING - 1 < groups)
        def _():
            start(group + RING - 1)

        for u in range(GROUP):
            copy(group, u).wait()
        slot = lax.rem(group, RING)
        products = []
        for u in range(GROUP):
            both = held[table[from_row, group * GROUP + u]]
            high, low = split(buf[slot, u])
            if transposed:
                p = dot(both, high, NN)
                products.append(p[:width] + p[width:] + dot(both[:width], low, NN))
            else:
                p = dot(both, jnp.concatenate([high, low], 0), NT)
                products.append(p[:width, :edge] + p[:width, edge:] + p[width:, :edge])
        for u in range(GROUP):
            to = table[to_row, group * GROUP + u]
            acc[to] = acc[to] + products[u]
        return carry

    lax.fori_loop(0, groups, step, 0)
    for b in range(n_out):
        for j in range(per):
            outs[b][:, j * edge : (j + 1) * edge] = acc[b * per + j]


def spmm(table, sources, values, n_out, transposed):
    n_in = len(sources)
    width, length = sources[0].shape
    slots, edge, _ = values.shape
    per = length // edge
    vmem = pl.BlockSpec(memory_space=pltpu.VMEM)
    return pl.pallas_call(
        functools.partial(spmm_kernel, transposed, n_in, n_out),
        in_specs=[pl.BlockSpec(memory_space=pltpu.SMEM)]
        + [vmem] * n_in
        + [pl.BlockSpec(memory_space=pl.ANY)],
        out_specs=[vmem] * n_out,
        out_shape=[jax.ShapeDtypeStruct((width, length), F32)] * n_out,
        scratch_shapes=[
            pltpu.VMEM((RING, GROUP, edge, edge), F32),
            pltpu.SemaphoreType.DMA((RING, GROUP)),
            pltpu.VMEM((n_in * per, 2 * width, edge), BF16),
            pltpu.VMEM((n_out * per + 1, width, edge), F32),
        ],
        compiler_params=pltpu.CompilerParams(vmem_limit_bytes=51 << 20),
        cost_estimate=pl.CostEstimate(
            flops=6 * slots * width * edge * edge, bytes_accessed=14 << 20, transcendentals=0
        ),
        name="spmm_back" if transposed else "spmm",
    )(table, *sources, values)


def mid_kernel(n_rep, place, *refs):
    aggs = refs[:n_rep]
    cots = refs[n_rep : 2 * n_rep]
    weight, weight_t, out, mixed_grad, grad_pre = refs[2 * n_rep : 2 * n_rep + 5]
    agg, cot, act = refs[2 * n_rep + 5 :]
    quarter = aggs[0].shape[0]
    me = place[0]
    for k in range(n_rep):
        at = pl.ds(pl.multiple_of((me ^ k) * quarter, quarter), quarter)
        agg[at, :] = aggs[k][...]
        cot[at, :] = cots[k][...]
    pre = dot3(weight_t[...], agg[...], NN)
    square = pre * pre
    curve = jnp.tanh(ROOT_2_PI * (pre + CUBIC * (square * pre)))
    half = 0.5 * (1.0 + curve)
    act[...] = pre * half
    slope = half + 0.5 * pre * (1.0 - curve * curve) * (
        ROOT_2_PI * (1.0 + 3.0 * CUBIC * square)
    )
    grad = cot[...] * slope
    grad_pre[...] = grad
    own = pl.ds(pl.multiple_of(me * quarter, quarter), quarter)
    mixed_grad[...] = dot3(weight[own, :], grad, NN)
    out[...] = act[own, :]


def mid(place, aggs, cots, weight, weight_t):
    n_rep = len(aggs)
    quarter, length = aggs[0].shape
    width = weight.shape[0]
    vmem = pl.BlockSpec(memory_space=pltpu.VMEM)
    return pl.pallas_call(
        functools.partial(mid_kernel, n_rep),
        in_specs=[pl.BlockSpec(memory_space=pltpu.SMEM)] + [vmem] * (2 * n_rep + 2),
        out_specs=[vmem] * 3,
        out_shape=[
            jax.ShapeDtypeStruct((quarter, length), F32),
            jax.ShapeDtypeStruct((quarter, length), F32),
            jax.ShapeDtypeStruct((width, length), F32),
        ],
        scratch_shapes=[pltpu.VMEM((width, length), F32)] * 3,
        compiler_params=pltpu.CompilerParams(vmem_limit_bytes=16 << 20),
        cost_estimate=pl.CostEstimate(
            flops=8 * width * width * length, bytes_accessed=4 << 20, transcendentals=0
        ),
        name="mid",
    )(place, *aggs, *cots, weight, weight_t)


def weight_kernel(scale, agg, grad_pre, out):
    out[...] = dot3(agg[...], grad_pre[...], NT) * scale


def weight_part(agg, grad_pre, scale):
    vmem = pl.BlockSpec(memory_space=pltpu.VMEM)
    return pl.pallas_call(
        functools.partial(weight_kernel, scale),
        in_specs=[vmem, vmem],
        out_specs=vmem,
        out_shape=jax.ShapeDtypeStruct((agg.shape[0], grad_pre.shape[0]), F32),
        compiler_params=pltpu.CompilerParams(vmem_limit_bytes=16 << 20),
        cost_estimate=pl.CostEstimate(
            flops=6 * agg.shape[0] * grad_pre.size, bytes_accessed=1 << 20, transcendentals=0
        ),
        name="weight_part",
    )(agg, grad_pre)


def shift(x, axis, by):
    n = lax.axis_size(axis)
    return lax.ppermute(x, axis, [(i, (i + by) % n) for i in range(n)])


def swap(x, axis, bit):
    n = lax.axis_size(axis)
    return lax.ppermute(x, axis, [(i, i ^ bit) for i in range(n)])


def layer(features, weight, cotangent, tile_values, tile_row, tile_col, tile_kind, tile_count):
    n_row, n_col, n_rep = (lax.axis_size(a) for a in ("row", "col", "rep"))
    row, col, rep = (lax.axis_index(a) for a in ("row", "col", "rep"))
    stretch = features.shape[1]
    per = stretch // tile_values.shape[1]
    slots = tile_kind.shape[0]

    def relative(tile, at, n):
        stretch_of = tile // per
        far = (stretch_of // 2 - at // 2) % (n // 2)
        return (far * 2 + ((stretch_of ^ at) & 1)) * per + tile % per

    live = jnp.arange(slots, dtype=jnp.int32) < tile_count[0]
    by_row = relative(tile_row, col, n_col)
    by_col = relative(tile_col, row, n_row)
    table = jnp.stack(
        [
            jnp.where(live, by_row, n_col * per),
            by_col,
            jnp.where(live, by_col, n_row * per),
            by_row,
            tile_kind,
            jnp.broadcast_to(tile_count, (slots,)),
        ]
    )
    blocks = []
    for k in range(n_row // 2):
        mine = features if k == 0 else shift(features, "row", -2 * k)
        blocks += [mine, swap(mine, "row", 1)]
    cots = [cotangent] + [swap(cotangent, "rep", k) for k in range(1, n_rep)]
    table, *cots[1:] = lax.optimization_barrier((table, *cots[1:]))
    parts = spmm(table, blocks, tile_values, n_col, False)
    sums = [None, None]
    for z in (1, 0):
        total = parts[z]
        for k in range(1, n_col // 2):
            total = total + shift(parts[2 * k + z], "col", 2 * k)
        sums[z] = total
    agg = sums[0] + swap(sums[1], "col", 1)
    aggs = [agg] + [swap(agg, "rep", k) for k in range(1, n_rep)]
    place = rep.astype(jnp.int32)[None]
    output, mixed_grad, grad_pre = mid(place, aggs, cots, weight, weight.T)
    far = swap(mixed_grad, "col", 1)
    blocks = [mixed_grad, far]
    for k in range(1, n_col // 2):
        blocks += [shift(mixed_grad, "col", -2 * k), shift(far, "col", -2 * k)]
    node_total = stretch * n_row * n_col
    weight_grad = weight_part(agg, grad_pre, float(node_total) ** (-0.5))

    def add_swapped(x, axis, bit):
        return x + swap(x, axis, bit)

    weight_grad = add_swapped(weight_grad, "row", 1)
    weight_grad = add_swapped(weight_grad, "row", 2)
    weight_grad = add_swapped(weight_grad, "row", 4)
    weight_grad = add_swapped(weight_grad, "col", 1)
    parts = spmm(table, blocks, tile_values, n_row, True)
    totals = [parts[2 * k] + swap(parts[2 * k + 1], "row", 1) for k in range(n_row // 2)]
    input_grad = totals[0]
    for k in (2, 1, 3):
        got = shift(totals[k], "row", 2 * k)
        input_grad = input_grad + got
    weight_grad = add_swapped(weight_grad, "col", 2)
    weight_grad = add_swapped(weight_grad, "col", 4)
    return (output, input_grad, weight_grad)


def solution(mesh):
    return jax.shard_map(
        layer,
        mesh=mesh,
        in_specs=(
            P("rep", ("col", "row")),
            P(),
            P("rep", ("row", "col")),
            P(("row", "col"), None, None),
            P(("row", "col")),
            P(("row", "col")),
            P(("row", "col")),
            P(("row", "col")),
        ),
        out_specs=(P("rep", ("row", "col")), P("rep", ("col", "row")), P("rep", None)),
        check_vma=False,
    )
```

```python
import functools

import jax
import jax.numpy as jnp
from jax import lax
from jax.experimental import pallas as pl
from jax.experimental.pallas import tpu as pltpu
from jax.sharding import PartitionSpec as P


BF16 = jnp.bfloat16
F32 = jnp.float32
NT = (((1,), (1,)), ((), ()))
NN = (((1,), (0,)), ((), ()))
GROUP = 16
ROOT_2_PI = 0.7978845608028654
CUBIC = 0.044715

dot = functools.partial(lax.dot_general, preferred_element_type=F32)


def split(x):
    high = x.astype(BF16)
    return high, (x - high.astype(F32)).astype(BF16)


def dot3(a, b, dims):
    a_high, a_low = split(a)
    b_high, b_low = split(b)
    return dot(a_high, b_high, dims) + dot(a_high, b_low, dims) + dot(a_low, b_high, dims)


def spmm_kernel(transposed, n_in, n_out, table, *refs):
    sources = refs[:n_in]
    values = refs[n_in]
    outs = refs[n_in + 1 : n_in + 1 + n_out]
    held, acc = refs[n_in + 1 + n_out :]
    width, length = sources[0].shape
    edge = values.shape[-1]
    per = length // edge
    to_row, from_row = (2, 3) if transposed else (0, 1)
    groups = (table[5, 0] + GROUP - 1) // GROUP

    for b in range(n_in):
        for j in range(per):
            high, low = split(sources[b][:, j * edge : (j + 1) * edge])
            held[b * per + j, :width] = high
            held[b * per + j, width:] = low
    acc[...] = jnp.zeros_like(acc)

    def step(group, carry):
        products = []
        for u in range(GROUP):
            both = held[table[from_row, group * GROUP + u]]
            high, low = split(values[table[4, group * GROUP + u]])
            if transposed:
                p = dot(both, high, NN)
                products.append(p[:width] + p[width:] + dot(both[:width], low, NN))
            else:
                p = dot(both, jnp.concatenate([high, low], 0), NT)
                products.append(p[:width, :edge] + p[:width, edge:] + p[width:, :edge])
        for u in range(GROUP):
            to = table[to_row, group * GROUP + u]
            acc[to] = acc[to] + products[u]
        return carry

    lax.fori_loop(0, groups, step, 0)
    for b in range(n_out):
        for j in range(per):
            outs[b][:, j * edge : (j + 1) * edge] = acc[b * per + j]


def spmm(table, sources, values, n_out, transposed):
    n_in = len(sources)
    width, length = sources[0].shape
    slots, edge, _ = values.shape
    per = length // edge
    vmem = pl.BlockSpec(memory_space=pltpu.VMEM)
    return pl.pallas_call(
        functools.partial(spmm_kernel, transposed, n_in, n_out),
        in_specs=[pl.BlockSpec(memory_space=pltpu.SMEM)]
        + [vmem] * n_in
        + [vmem],
        out_specs=[vmem] * n_out,
        out_shape=[jax.ShapeDtypeStruct((width, length), F32)] * n_out,
        scratch_shapes=[
            pltpu.VMEM((n_in * per, 2 * width, edge), BF16),
            pltpu.VMEM((n_out * per + 1, width, edge), F32),
        ],
        compiler_params=pltpu.CompilerParams(vmem_limit_bytes=24 << 20),
        cost_estimate=pl.CostEstimate(
            flops=6 * slots * width * edge * edge, bytes_accessed=14 << 20, transcendentals=0
        ),
        name="spmm_back" if transposed else "spmm",
    )(table, *sources, values)


def mid_kernel(n_rep, place, *refs):
    aggs = refs[:n_rep]
    cots = refs[n_rep : 2 * n_rep]
    weight, weight_t, out, mixed_grad, grad_pre = refs[2 * n_rep : 2 * n_rep + 5]
    agg, cot, act = refs[2 * n_rep + 5 :]
    quarter = aggs[0].shape[0]
    me = place[0]
    for k in range(n_rep):
        at = pl.ds(pl.multiple_of((me ^ k) * quarter, quarter), quarter)
        agg[at, :] = aggs[k][...]
        cot[at, :] = cots[k][...]
    pre = dot3(weight_t[...], agg[...], NN)
    square = pre * pre
    curve = jnp.tanh(ROOT_2_PI * (pre + CUBIC * (square * pre)))
    half = 0.5 * (1.0 + curve)
    act[...] = pre * half
    slope = half + 0.5 * pre * (1.0 - curve * curve) * (
        ROOT_2_PI * (1.0 + 3.0 * CUBIC * square)
    )
    grad = cot[...] * slope
    grad_pre[...] = grad
    own = pl.ds(pl.multiple_of(me * quarter, quarter), quarter)
    mixed_grad[...] = dot3(weight[own, :], grad, NN)
    out[...] = act[own, :]


def mid(place, aggs, cots, weight, weight_t):
    n_rep = len(aggs)
    quarter, length = aggs[0].shape
    width = weight.shape[0]
    vmem = pl.BlockSpec(memory_space=pltpu.VMEM)
    return pl.pallas_call(
        functools.partial(mid_kernel, n_rep),
        in_specs=[pl.BlockSpec(memory_space=pltpu.SMEM)] + [vmem] * (2 * n_rep + 2),
        out_specs=[vmem] * 3,
        out_shape=[
            jax.ShapeDtypeStruct((quarter, length), F32),
            jax.ShapeDtypeStruct((quarter, length), F32),
            jax.ShapeDtypeStruct((width, length), F32),
        ],
        scratch_shapes=[pltpu.VMEM((width, length), F32)] * 3,
        compiler_params=pltpu.CompilerParams(vmem_limit_bytes=16 << 20),
        cost_estimate=pl.CostEstimate(
            flops=8 * width * width * length, bytes_accessed=4 << 20, transcendentals=0
        ),
        name="mid",
    )(place, *aggs, *cots, weight, weight_t)


def weight_kernel(scale, agg, grad_pre, out):
    out[...] = dot3(agg[...], grad_pre[...], NT) * scale


def weight_part(agg, grad_pre, scale):
    vmem = pl.BlockSpec(memory_space=pltpu.VMEM)
    return pl.pallas_call(
        functools.partial(weight_kernel, scale),
        in_specs=[vmem, vmem],
        out_specs=vmem,
        out_shape=jax.ShapeDtypeStruct((agg.shape[0], grad_pre.shape[0]), F32),
        compiler_params=pltpu.CompilerParams(vmem_limit_bytes=16 << 20),
        cost_estimate=pl.CostEstimate(
            flops=6 * agg.shape[0] * grad_pre.size, bytes_accessed=1 << 20, transcendentals=0
        ),
        name="weight_part",
    )(agg, grad_pre)


def shift(x, axis, by):
    n = lax.axis_size(axis)
    return lax.ppermute(x, axis, [(i, (i + by) % n) for i in range(n)])


def swap(x, axis, bit):
    n = lax.axis_size(axis)
    return lax.ppermute(x, axis, [(i, i ^ bit) for i in range(n)])


def layer(features, weight, cotangent, tile_values, tile_row, tile_col, tile_kind, tile_count):
    n_row, n_col, n_rep = (lax.axis_size(a) for a in ("row", "col", "rep"))
    row, col, rep = (lax.axis_index(a) for a in ("row", "col", "rep"))
    stretch = features.shape[1]
    per = stretch // tile_values.shape[1]
    slots = tile_kind.shape[0]

    def relative(tile, at, n):
        stretch_of = tile // per
        far = (stretch_of // 2 - at // 2) % (n // 2)
        return (far * 2 + ((stretch_of ^ at) & 1)) * per + tile % per

    live = jnp.arange(slots, dtype=jnp.int32) < tile_count[0]
    by_row = relative(tile_row, col, n_col)
    by_col = relative(tile_col, row, n_row)
    table = jnp.stack(
        [
            jnp.where(live, by_row, n_col * per),
            by_col,
            jnp.where(live, by_col, n_row * per),
            by_row,
            tile_kind,
            jnp.broadcast_to(tile_count, (slots,)),
        ]
    )
    blocks = []
    for k in range(n_row // 2):
        mine = features if k == 0 else shift(features, "row", -2 * k)
        blocks += [mine, swap(mine, "row", 1)]
    cots = [cotangent]
    for k in range(1, n_rep):
        cots.append(swap(cotangent, "rep", k))
    parts = spmm(table, blocks, tile_values, n_col, False)
    sums = [None, None]
    for z in (1, 0):
        total = parts[z]
        for k in range(1, n_col // 2):
            got = shift(parts[2 * k + z], "col", 2 * k)
            total = total + got
        sums[z] = total
    far = swap(sums[1], "col", 1)
    agg = sums[0] + far
    aggs = [agg] + [swap(agg, "rep", k) for k in range(1, n_rep)]
    place = rep.astype(jnp.int32)[None]
    output, mixed_grad, grad_pre = mid(place, aggs, cots, weight, weight.T)
    far = swap(mixed_grad, "col", 1)
    blocks = [mixed_grad, far]
    for k in range(1, n_col // 2):
        blocks.append(shift(mixed_grad, "col", -2 * k))
        blocks.append(shift(far, "col", -2 * k))
    node_total = stretch * n_row * n_col
    weight_grad = weight_part(agg, grad_pre, float(node_total) ** (-0.5))

    def add_swapped(x, axis, bit):
        return x + swap(x, axis, bit)

    weight_grad = add_swapped(weight_grad, "row", 1)
    weight_grad = add_swapped(weight_grad, "row", 2)
    weight_grad = add_swapped(weight_grad, "row", 4)
    weight_grad = add_swapped(weight_grad, "col", 1)
    parts = spmm(table, blocks, tile_values, n_row, True)
    totals = [parts[2 * k] + swap(parts[2 * k + 1], "row", 1) for k in range(n_row // 2)]
    input_grad = totals[0]
    for k in (2, 1, 3):
        got = shift(totals[k], "row", 2 * k)
        input_grad = input_grad + got
    weight_grad = add_swapped(weight_grad, "col", 2)
    weight_grad = add_swapped(weight_grad, "col", 4)
    return (output, input_grad, weight_grad)


def solution(mesh):
    return jax.shard_map(
        layer,
        mesh=mesh,
        in_specs=(
            P("rep", ("col", "row")),
            P(),
            P("rep", ("row", "col")),
            P(("row", "col"), None, None),
            P(("row", "col")),
            P(("row", "col")),
            P(("row", "col")),
            P(("row", "col")),
        ),
        out_specs=(P("rep", ("row", "col")), P("rep", ("col", "row")), P("rep", None)),
        check_vma=False,
    )
```

```python
import functools
import math

import jax
import jax.numpy as jnp
from jax import lax
from jax.experimental import pallas as pl
from jax.experimental.pallas import tpu as pltpu
from jax.sharding import PartitionSpec as P


BF16 = jnp.bfloat16
F32 = jnp.float32
NT = (((1,), (1,)), ((), ()))
NN = (((1,), (0,)), ((), ()))
GROUP = 16
RING = 4
ROOT_2_PI = 0.7978845608028654
CUBIC = 0.044715
SMALL = 16 << 20

dot = functools.partial(lax.dot_general, preferred_element_type=F32)


def split(x):
    high = x.astype(BF16)
    return high, (x - high.astype(F32)).astype(BF16)


def dot3(a, b, dims):
    a_high, a_low = split(a)
    b_high, b_low = split(b)
    return dot(a_high, b_high, dims) + dot(a_high, b_low, dims) + dot(a_low, b_high, dims)


def spmm_kernel(transposed, n_in, n_out, table, *refs):
    sources = refs[:n_in]
    values = refs[n_in]
    outs = refs[n_in + 1 : n_in + 1 + n_out]
    buf, sem, held, acc = refs[n_in + 1 + n_out :]
    edge = values.shape[-1]
    width = acc.shape[1]
    to_row, from_row = (2, 3) if transposed else (0, 1)
    groups = (table[5, 0] + GROUP - 1) // GROUP

    def copy(group, u):
        slot = lax.rem(group, RING)
        return pltpu.make_async_copy(
            values.at[table[4, group * GROUP + u]], buf.at[slot, u], sem.at[slot, u]
        )

    def start(group):
        def one(u, carry):
            copy(group, u).start()
            return carry

        lax.fori_loop(0, GROUP, one, 0, unroll=4)

    for g in range(RING - 1):

        @pl.when(g < groups)
        def _():
            start(g)

    per = held.shape[0] // n_in
    for b in range(n_in):
        for j in range(per):
            ref = sources[b]
            tile = ref[:, j * edge : (j + 1) * edge] if ref.ndim == 2 else ref[j]
            high, low = split(tile)
            held[b * per + j, :width] = high
            held[b * per + j, width:] = low
    acc[...] = jnp.zeros_like(acc)

    def step(group, carry):
        @pl.when(group + RING - 1 < groups)
        def _():
            start(group + RING - 1)

        for u in range(GROUP):
            copy(group, u).wait()
        slot = lax.rem(group, RING)
        products = []
        for u in range(GROUP):
            both = held[table[from_row, group * GROUP + u]]
            high, low = split(buf[slot, u])
            if transposed:
                p = dot(both, high, NN)
                products.append(p[:width] + p[width:] + dot(both[:width], low, NN))
            else:
                p = dot(both, jnp.concatenate([high, low], 0), NT)
                products.append(p[:width, :edge] + p[:width, edge:] + p[width:, :edge])
        for u in range(GROUP):
            to = table[to_row, group * GROUP + u]
            acc[to] = acc[to] + products[u]
        return carry

    lax.fori_loop(0, groups, step, 0)
    per = acc.shape[0] // n_out
    for b in range(n_out):
        for j in range(per):
            if outs[b].ndim == 2:
                outs[b][:, j * edge : (j + 1) * edge] = acc[b * per + j]
            else:
                outs[b][j] = acc[b * per + j]


def spmm(table, sources, values, n_from, n_out, out_shape, width, transposed):
    n_in = len(sources)
    slots, edge, _ = values.shape
    n_to = n_out * math.prod(out_shape) // (width * edge)
    vmem = pl.BlockSpec(memory_space=pltpu.VMEM)
    return pl.pallas_call(
        functools.partial(spmm_kernel, transposed, n_in, n_out),
        in_specs=[pl.BlockSpec(memory_space=pltpu.SMEM)]
        + [vmem] * n_in
        + [pl.BlockSpec(memory_space=pl.ANY)],
        out_specs=[vmem] * n_out,
        out_shape=[jax.ShapeDtypeStruct(out_shape, F32)] * n_out,
        scratch_shapes=[
            pltpu.VMEM((RING, GROUP, edge, edge), F32),
            pltpu.SemaphoreType.DMA((RING, GROUP)),
            pltpu.VMEM((n_from, 2 * width, edge), BF16),
            pltpu.VMEM((n_to + 1, width, edge), F32),
        ],
        compiler_params=pltpu.CompilerParams(vmem_limit_bytes=51 << 20),
        cost_estimate=pl.CostEstimate(
            flops=6 * slots * width * edge * edge, bytes_accessed=14 << 20, transcendentals=0
        ),
        name="spmm_back" if transposed else "spmm",
    )(table, *sources, values)


def small(body, out_shapes, *args, scalars=1, scratch=(), flops=1 << 20):
    vmem = pl.BlockSpec(memory_space=pltpu.VMEM)
    call = pl.pallas_call(
        body,
        in_specs=[pl.BlockSpec(memory_space=pltpu.SMEM)] * scalars
        + [vmem] * (len(args) - scalars),
        out_specs=[vmem] * len(out_shapes),
        out_shape=[jax.ShapeDtypeStruct(shape, F32) for shape in out_shapes],
        scratch_shapes=[pltpu.VMEM(shape, F32) for shape in scratch],
        compiler_params=pltpu.CompilerParams(vmem_limit_bytes=SMALL),
        cost_estimate=pl.CostEstimate(flops=flops, bytes_accessed=1 << 20, transcendentals=0),
    )
    return list(call(*args))


def part(n, size, index):
    return pl.ds(pl.multiple_of(lax.rem(index + 2 * n, n) * size, size), size)


def cut_kernel(place, whole, *outs):
    n = len(outs)
    size = whole.shape[1] // n
    for d in range(n):
        outs[d][...] = whole[:, part(n, size, place[0] + d)]


def join_kernel(place, *refs):
    out = refs[-1]
    n = len(refs) - 1
    size = out.shape[1] // n
    for d in range(n):
        out[:, part(n, size, place[0] - d)] = refs[d][...]


def fold_kernel(n, *refs):
    for i in range(refs[0].shape[0]):
        total = refs[0][i]
        for k in range(1, n):
            total = total + refs[k][i]
        refs[n + i][...] = total


def stack_kernel(*refs):
    out = refs[-1]
    n = len(refs) - 1
    for i in range(n):
        out[i] = refs[i][0]
    for j in range(1, refs[0].shape[0]):
        total = refs[0][j]
        for i in range(1, n):
            total = total + refs[i][j]
        out[n + j - 1] = total


def tail_kernel(first, *refs):
    out = refs[-1]
    for j in range(out.shape[0]):
        total = refs[0][first + j]
        for ref in refs[1:-1]:
            total = total + ref[first + j]
        out[j] = total


def mid_kernel(n_rep, n_z, scale, place, *refs):
    sums = refs[:n_z]
    cots = refs[n_z : n_z + n_rep]
    weight, weight_t = refs[n_z + n_rep : n_z + n_rep + 2]
    refs = refs[n_z + n_rep + 2 :]
    grads = refs[:n_rep]
    acts = refs[n_rep : 2 * n_rep]
    agg, cot, act, mixed_grad, weight_grad = refs[2 * n_rep :]
    quarter, edge = sums[0].shape
    me = place[0]
    for d in range(n_rep):
        total = sums[d][...]
        for e in range(d + n_rep, n_z, n_rep):
            total = total + sums[e][...]
        agg[part(n_rep, quarter, me - d), :] = total
        cot[part(n_rep, quarter, me - d), :] = cots[d][...]
    pre = dot3(weight_t[...], agg[...], NN)
    square = pre * pre
    curve = jnp.tanh(ROOT_2_PI * (pre + CUBIC * (square * pre)))
    half = 0.5 * (1.0 + curve)
    act[...] = pre * half
    slope = half + 0.5 * pre * (1.0 - curve * curve) * (
        ROOT_2_PI * (1.0 + 3.0 * CUBIC * square)
    )
    grad = cot[...] * slope
    mixed_grad[...] = dot3(weight[...], grad, NN)
    weight_grad[...] = dot3(agg[...], grad, NT) * scale
    for d in range(n_rep):
        at = part(n_rep, quarter, me + d)
        grads[d][0] = mixed_grad[at, :]
        for j in range(1, grads[d].shape[0]):
            grads[d][j] = weight_grad[at, (j - 1) * edge : j * edge]
        acts[d][...] = act[at, :]


def shift(x, axis, by):
    n = lax.axis_size(axis)
    return lax.ppermute(x, axis, [(i, (i + by) % n) for i in range(n)])


def shift_z(x, by):
    n = lax.axis_size(("col", "rep"))
    m = 2 * lax.axis_size("rep")
    return lax.ppermute(x, ("col", "rep"), [(i, i // m * m + (i + by) % m) for i in range(n)])


def swap(x, axis, bit):
    n = lax.axis_size(axis)
    return lax.ppermute(x, axis, [(i, i ^ bit) for i in range(n)])


def layer(features, weight, cotangent, tile_values, tile_row, tile_col, tile_kind, tile_count):
    n_row, n_col, n_rep = (lax.axis_size(a) for a in ("row", "col", "rep"))
    row, col, rep = (lax.axis_index(a) for a in ("row", "col", "rep"))
    n_x, n_y, n_z = n_col // 2, n_row // 2, 2 * n_rep
    width, stretch = features.shape
    edge = tile_values.shape[1]
    per = stretch // edge
    slots = tile_kind.shape[0]
    full = weight.shape[0]
    z = (col & 1) * n_rep + rep
    place = rep.astype(jnp.int32)[None]

    far_x = ((tile_row // n_z - col // 2) & (n_x - 1)) * n_z
    at_z = tile_row & (n_z - 1)
    stretch_of = tile_col // per
    far_y = (stretch_of // 2 - row // 2) & (n_y - 1)
    by_col = (far_y * 2 + ((stretch_of ^ row) & 1)) * per + (tile_col & (per - 1))
    live = jnp.arange(slots, dtype=jnp.int32) < tile_count[0]
    table = jnp.stack(
        [
            jnp.where(live, far_x + ((at_z - z) & (n_z - 1)), n_x * n_z),
            by_col,
            jnp.where(live, by_col, n_row * per),
            far_x + ((z - at_z) & (n_z - 1)),
            tile_kind,
            jnp.broadcast_to(tile_count, (slots,)),
        ]
    )
    blocks = []
    for k in range(n_y):
        x = shift(features, "row", -2 * k) if k else features
        blocks += [x, swap(x, "row", 1)]
    pieces = small(cut_kernel, [(width, edge)] * n_rep, place, cotangent)
    cots = pieces[:1]
    for d in range(1, n_rep):
        cots.append(shift(pieces[d], "rep", d))
    parts = spmm(
        table, blocks, tile_values, n_row * per, n_x, (n_z, width, edge), width, False
    )
    got = [parts[0]] + [shift(parts[k], "col", 2 * k) for k in range(1, n_x)]
    sums = small(
        functools.partial(fold_kernel, n_x),
        [(width, edge)] * n_z, *got, scalars=0,
    )
    for d in range(1, n_z):
        sums[d] = shift_z(sums[d], d)
    scale = float(stretch * n_row * n_col) ** (-0.5)
    extra = full // edge
    outs = small(
        functools.partial(mid_kernel, n_rep, n_z, scale),
        [(1 + extra, width, edge)] * n_rep + [(width, edge)] * n_rep,
        place, *sums, *cots, weight, weight.T,
        scratch=[(full, edge)] * 4 + [(full, full)], flops=18 * full * full * edge,
    )
    grads, acts = outs[:n_rep], outs[n_rep:]
    pieces = grads[:1]
    for d in range(1, n_z):
        pieces.append(shift_z(grads[d % n_rep], d))
    blocks = small(stack_kernel, [(n_z + extra, width, edge)], *pieces, scalars=0)
    for k in range(1, n_x):
        blocks.append(shift(blocks[0], "col", -2 * k))
    (weight_grad,) = small(
        functools.partial(tail_kernel, n_z),
        [(extra, width, edge)], *blocks, scalars=0,
    )

    def add_swapped(x, axis, bit):
        return x + swap(x, axis, bit)

    weight_grad = add_swapped(weight_grad, "row", 1)
    for d in range(1, n_rep):
        acts[d] = shift(acts[d], "rep", d)
    (output,) = small(join_kernel, [(width, stretch)], place, *acts)
    parts = spmm(
        table, blocks, tile_values, n_x * n_z, n_row, (width, stretch), width, True
    )
    totals = [parts[2 * k] + swap(parts[2 * k + 1], "row", 1) for k in range(n_y)]
    input_grad = totals[0]
    for k in (2, 1, 3):
        got = shift(totals[k], "row", 2 * k)
        input_grad = input_grad + got
    weight_grad = add_swapped(weight_grad, "row", 2)
    weight_grad = add_swapped(weight_grad, "row", 4)
    weight_grad = jnp.concatenate([weight_grad[j] for j in range(extra)], axis=1)
    return (output, input_grad, weight_grad)


def solution(mesh):
    return jax.shard_map(
        layer,
        mesh=mesh,
        in_specs=(
            P("rep", ("col", "row")),
            P(),
            P("rep", ("row", "col")),
            P(("row", "col"), None, None),
            P(("row", "col")),
            P(("row", "col")),
            P(("row", "col")),
            P(("row", "col")),
        ),
        out_specs=(P("rep", ("row", "col")), P("rep", ("col", "row")), P("rep", None)),
        check_vma=False,
    )
```

```python
import functools

import jax
import jax.numpy as jnp
from jax import lax
from jax.experimental import pallas as pl
from jax.experimental.pallas import tpu as pltpu
from jax.sharding import PartitionSpec as P


BF16 = jnp.bfloat16
F32 = jnp.float32
NT = (((1,), (1,)), ((), ()))
NN = (((1,), (0,)), ((), ()))
GROUP = 16
CHUNK = 16
BITS = 5
ROOT_2_PI = 0.7978845608028654
CUBIC = 0.044715

dot = functools.partial(lax.dot_general, preferred_element_type=F32)


def split(x):
    high = x.astype(BF16)
    return high, (x - high.astype(F32)).astype(BF16)


def dot3(a, b, dims):
    a_high, a_low = split(a)
    b_high, b_low = split(b)
    return dot(a_high, b_high, dims) + dot(a_high, b_low, dims) + dot(a_low, b_high, dims)


def spmm_kernel(transposed, n_in, n_out, table, *refs):
    sources = refs[:n_in]
    values = refs[n_in]
    outs = refs[n_in + 1 : n_in + 1 + n_out]
    tiles, tile_sem, held, acc = refs[n_in + 1 + n_out :]
    width, length = sources[0].shape
    slots, edge, _ = values.shape
    per = length // edge
    chunks = slots // CHUNK
    count = table[slots]
    groups = (count + GROUP - 1) // GROUP

    def copy(chunk):
        at = pl.ds(chunk * CHUNK, CHUNK)
        return pltpu.make_async_copy(values.at[at], tiles.at[at], tile_sem.at[chunk])

    for c in range(chunks):
        copy(c).start()

    for b in range(n_in):
        ref = sources[b]
        for j in range(per):
            high, low = split(ref[:, j * edge : (j + 1) * edge])
            held[b * per + j, :width] = high
            held[b * per + j, width:] = low
    acc[...] = jnp.zeros_like(acc)

    def wait(chunk, carry):
        copy(chunk).wait()
        return carry

    def step(group, here):
        last = table[jnp.minimum(group * GROUP + GROUP, count) - 1]
        need = (last >> 2 * BITS) // CHUNK + 1
        lax.fori_loop(here, need, wait, 0)
        places = []
        products = []
        for u in range(GROUP):
            slot = group * GROUP + u
            packed = table[jnp.minimum(slot, count - 1)]
            kind = packed >> 2 * BITS
            by_row = (packed >> BITS) & (2**BITS - 1)
            by_col = packed & (2**BITS - 1)
            to, at = (by_col, by_row) if transposed else (by_row, by_col)
            places.append(jnp.where(slot < count, to, n_out * per))
            both = held[at]
            high, low = split(tiles[kind])
            if transposed:
                p = dot(both, high, NN)
                products.append(p[:width] + p[width:] + dot(both[:width], low, NN))
            else:
                p = dot(both, jnp.concatenate([high, low], 0), NT)
                products.append(p[:width, :edge] + p[:width, edge:] + p[width:, :edge])
        for u in range(GROUP):
            acc[places[u]] = acc[places[u]] + products[u]
        return jnp.maximum(here, need)

    here = lax.fori_loop(0, groups, step, 0)
    lax.fori_loop(here, chunks, wait, 0)
    for b in range(n_out):
        for j in range(per):
            outs[b][:, j * edge : (j + 1) * edge] = acc[b * per + j]


def spmm(table, sources, values, n_out, transposed):
    n_in = len(sources)
    width, length = sources[0].shape
    slots, edge, _ = values.shape
    per = length // edge
    vmem = pl.BlockSpec(memory_space=pltpu.VMEM)
    anywhere = pl.BlockSpec(memory_space=pl.ANY)
    return pl.pallas_call(
        functools.partial(spmm_kernel, transposed, n_in, n_out),
        in_specs=[pl.BlockSpec(memory_space=pltpu.SMEM)] + [vmem] * n_in + [anywhere],
        out_specs=[vmem] * n_out,
        out_shape=[jax.ShapeDtypeStruct((width, length), F32)] * n_out,
        scratch_shapes=[
            pltpu.VMEM((slots, edge, edge), F32),
            pltpu.SemaphoreType.DMA((slots // CHUNK,)),
            pltpu.VMEM((n_in * per, 2 * width, edge), BF16),
            pltpu.VMEM((n_out * per + 1, width, edge), F32),
        ],
        compiler_params=pltpu.CompilerParams(vmem_limit_bytes=51 << 20),
        cost_estimate=pl.CostEstimate(
            flops=6 * slots * width * edge * edge, bytes_accessed=14 << 20, transcendentals=0
        ),
        name="spmm_back" if transposed else "spmm",
    )(table, *sources, values)


def stage_kernel(source, out):
    out[...] = source[...]


def stage(x):
    vmem = pl.BlockSpec(memory_space=pltpu.VMEM)
    return pl.pallas_call(
        stage_kernel,
        in_specs=[vmem],
        out_specs=vmem,
        out_shape=jax.ShapeDtypeStruct(x.shape, x.dtype),
        compiler_params=pltpu.CompilerParams(vmem_limit_bytes=4 << 20),
        cost_estimate=pl.CostEstimate(flops=0, bytes_accessed=1 << 18, transcendentals=0),
        name="stage",
    )(x)


def mid_kernel(n_rep, scale, place, *refs):
    aggs = refs[:n_rep]
    cots = refs[n_rep : 2 * n_rep]
    weight, weight_t, out, mixed_grad, sent = refs[2 * n_rep : 2 * n_rep + 5]
    agg, cot, act = refs[2 * n_rep + 5 :]
    quarter = aggs[0].shape[0]
    me = place[0]
    for k in range(n_rep):
        at = pl.ds(pl.multiple_of((me ^ k) * quarter, quarter), quarter)
        agg[at, :] = aggs[k][...]
        cot[at, :] = cots[k][...]
    pre = dot3(weight_t[...], agg[...], NN)
    square = pre * pre
    curve = jnp.tanh(ROOT_2_PI * (pre + CUBIC * (square * pre)))
    half = 0.5 * (1.0 + curve)
    act[...] = pre * half
    slope = half + 0.5 * pre * (1.0 - curve * curve) * (
        ROOT_2_PI * (1.0 + 3.0 * CUBIC * square)
    )
    grad = cot[...] * slope
    own = pl.ds(pl.multiple_of(me * quarter, quarter), quarter)
    mine = dot3(weight[own, :], grad, NN)
    length = mine.shape[1]
    mixed_grad[...] = mine
    sent[:, :length] = mine
    sent[:, length:] = dot3(agg[own, :], grad, NT) * scale
    out[...] = act[own, :]


def mid(place, aggs, cots, weight, weight_t, scale):
    n_rep = len(aggs)
    quarter, length = aggs[0].shape
    width = weight.shape[0]
    vmem = pl.BlockSpec(memory_space=pltpu.VMEM)
    return pl.pallas_call(
        functools.partial(mid_kernel, n_rep, scale),
        in_specs=[pl.BlockSpec(memory_space=pltpu.SMEM)] + [vmem] * (2 * n_rep + 2),
        out_specs=[vmem] * 3,
        out_shape=[
            jax.ShapeDtypeStruct((quarter, length), F32),
            jax.ShapeDtypeStruct((quarter, length), F32),
            jax.ShapeDtypeStruct((quarter, length + width), F32),
        ],
        scratch_shapes=[pltpu.VMEM((width, length), F32)] * 3,
        compiler_params=pltpu.CompilerParams(vmem_limit_bytes=16 << 20),
        cost_estimate=pl.CostEstimate(
            flops=8 * width * width * length, bytes_accessed=4 << 20, transcendentals=0
        ),
        name="mid",
    )(place, *aggs, *cots, weight, weight_t)


def shift(x, axis, by):
    n = lax.axis_size(axis)
    return lax.ppermute(x, axis, [(i, (i + by) % n) for i in range(n)])


def swap(x, axis, bit):
    n = lax.axis_size(axis)
    return lax.ppermute(x, axis, [(i, i ^ bit) for i in range(n)])


def layer(features, weight, cotangent, tile_values, tile_row, tile_col, tile_kind, tile_count):
    n_row, n_col, n_rep = (lax.axis_size(a) for a in ("row", "col", "rep"))
    row, col, rep = (lax.axis_index(a) for a in ("row", "col", "rep"))
    stretch = features.shape[1]
    per = stretch // tile_values.shape[1]
    slots = tile_kind.shape[0]

    def relative(tile, at, n):
        stretch_of = tile // per
        far = (stretch_of // 2 - at // 2) % (n // 2)
        return (far * 2 + ((stretch_of ^ at) & 1)) * per + tile % per

    by_row = relative(tile_row, col, n_col)
    by_col = relative(tile_col, row, n_row)
    ids = jnp.arange(slots, dtype=jnp.int32)
    packed = (tile_kind << 2 * BITS) + (by_row << BITS) + by_col
    key = jnp.where(ids < tile_count[0], tile_kind, slots) * slots + ids
    rank = jnp.sum((key[None, :] < key[:, None]).astype(jnp.int32), axis=1)
    ordered = jnp.sum(jnp.where(rank[None, :] == ids[:, None], packed[None, :], 0), axis=1)
    table = jnp.concatenate([ordered, tile_count])
    blocks = []
    for k in range(n_row // 2):
        mine = shift(features, "row", -2 * k) if k else features
        blocks += [mine, swap(mine, "row", 1)]
    blocks[0] = stage(features)
    cots = [cotangent]
    for k in range(1, n_rep):
        cots.append(swap(cotangent, "rep", k))
    parts = spmm(table, blocks, tile_values, n_col, False)
    sums = [None, None]
    for z in (1, 0):
        total = parts[z]
        for k in range(1, n_col // 2):
            got = shift(parts[2 * k + z], "col", 2 * k)
            total = total + got
        sums[z] = total
    far = swap(sums[1], "col", 1)
    agg = sums[0] + far
    aggs = [agg] + [swap(agg, "rep", k) for k in range(1, n_rep)]
    place = rep.astype(jnp.int32)[None]
    node_total = stretch * n_row * n_col
    output, mixed_grad, sent = mid(
        place, aggs, cots, weight, weight.T, float(node_total) ** (-0.5)
    )
    far = swap(mixed_grad, "col", 1)
    blocks = [mixed_grad, far]
    weight_grad = sent[:, stretch:]
    for k in range(1, n_col // 2):
        got = shift(sent, "col", -2 * k)
        weight_grad = weight_grad + got[:, stretch:]
        blocks += [got, shift(far, "col", -2 * k)]

    def add_swapped(x, axis, bit):
        return x + swap(x, axis, bit)

    weight_grad = add_swapped(weight_grad, "col", 1)
    parts = spmm(table, blocks, tile_values, n_row, True)
    totals = []
    for k in range(n_row // 2):
        got = swap(parts[2 * k + 1], "row", 1)
        totals.append(parts[2 * k] + got)
    input_grad = totals[0]
    for k in (2, 1, 3):
        got = shift(totals[k], "row", 2 * k)
        input_grad = input_grad + got
    weight_grad = add_swapped(weight_grad, "row", 1)
    weight_grad = add_swapped(weight_grad, "row", 2)
    weight_grad = add_swapped(weight_grad, "row", 4)
    return (output, input_grad, weight_grad)


def solution(mesh):
    return jax.shard_map(
        layer,
        mesh=mesh,
        in_specs=(
            P("rep", ("col", "row")),
            P(),
            P("rep", ("row", "col")),
            P(("row", "col"), None, None),
            P(("row", "col")),
            P(("row", "col")),
            P(("row", "col")),
            P(("row", "col")),
        ),
        out_specs=(P("rep", ("row", "col")), P("rep", ("col", "row")), P("rep", None)),
        check_vma=False,
    )
```

```python
import functools

import jax
import jax.numpy as jnp
from jax import lax
from jax.experimental import pallas as pl
from jax.experimental.pallas import tpu as pltpu
from jax.sharding import PartitionSpec as P


BF16 = jnp.bfloat16
F32 = jnp.float32
NT = (((1,), (1,)), ((), ()))
NN = (((1,), (0,)), ((), ()))
GROUP = 16
CHUNK = 16
BITS = 5
ROOT_2_PI = 0.7978845608028654
CUBIC = 0.044715

dot = functools.partial(lax.dot_general, preferred_element_type=F32)


def split(x):
    high = x.astype(BF16)
    return high, (x - high.astype(F32)).astype(BF16)


def dot3(a, b, dims):
    a_high, a_low = split(a)
    b_high, b_low = split(b)
    return dot(a_high, b_high, dims) + dot(a_high, b_low, dims) + dot(a_low, b_high, dims)


def spmm_kernel(transposed, n_in, n_out, table, *refs):
    sources = refs[:n_in]
    values = refs[n_in]
    outs = refs[n_in + 1 : n_in + 1 + n_out]
    tiles, tile_sem, held, acc = refs[n_in + 1 + n_out :]
    width, length = sources[0].shape
    slots, edge, _ = values.shape
    per = length // edge
    chunks = slots // CHUNK
    count = table[slots]
    groups = (count + GROUP - 1) // GROUP

    def copy(chunk):
        at = pl.ds(chunk * CHUNK, CHUNK)
        return pltpu.make_async_copy(values.at[at], tiles.at[at], tile_sem.at[chunk])

    for c in range(chunks):
        copy(c).start()

    for b in range(n_in):
        ref = sources[b]
        for j in range(per):
            high, low = split(ref[:, j * edge : (j + 1) * edge])
            held[b * per + j, :width] = high
            held[b * per + j, width:] = low
    acc[...] = jnp.zeros_like(acc)

    def wait(chunk, carry):
        copy(chunk).wait()
        return carry

    def step(group, here):
        last = table[jnp.minimum(group * GROUP + GROUP, count) - 1]
        need = (last >> 2 * BITS) // CHUNK + 1
        lax.fori_loop(here, need, wait, 0)
        places = []
        products = []
        for u in range(GROUP):
            slot = group * GROUP + u
            packed = table[jnp.minimum(slot, count - 1)]
            kind = packed >> 2 * BITS
            by_row = (packed >> BITS) & (2**BITS - 1)
            by_col = packed & (2**BITS - 1)
            to, at = (by_col, by_row) if transposed else (by_row, by_col)
            places.append(jnp.where(slot < count, to, n_out * per))
            both = held[at]
            high, low = split(tiles[kind])
            if transposed:
                p = dot(both, high, NN)
                products.append(p[:width] + p[width:] + dot(both[:width], low, NN))
            else:
                p = dot(both, jnp.concatenate([high, low], 0), NT)
                products.append(p[:width, :edge] + p[:width, edge:] + p[width:, :edge])
        for u in range(GROUP):
            acc[places[u]] = acc[places[u]] + products[u]
        return jnp.maximum(here, need)

    here = lax.fori_loop(0, groups, step, 0)
    lax.fori_loop(here, chunks, wait, 0)
    for b in range(n_out):
        for j in range(per):
            outs[b][:, j * edge : (j + 1) * edge] = acc[b * per + j]


def spmm(table, sources, values, n_out, transposed):
    n_in = len(sources)
    width, length = sources[0].shape
    slots, edge, _ = values.shape
    per = length // edge
    vmem = pl.BlockSpec(memory_space=pltpu.VMEM)
    anywhere = pl.BlockSpec(memory_space=pl.ANY)
    return pl.pallas_call(
        functools.partial(spmm_kernel, transposed, n_in, n_out),
        in_specs=[pl.BlockSpec(memory_space=pltpu.SMEM)] + [vmem] * n_in + [anywhere],
        out_specs=[vmem] * n_out,
        out_shape=[jax.ShapeDtypeStruct((width, length), F32)] * n_out,
        scratch_shapes=[
            pltpu.VMEM((slots, edge, edge), F32),
            pltpu.SemaphoreType.DMA((slots // CHUNK,)),
            pltpu.VMEM((n_in * per, 2 * width, edge), BF16),
            pltpu.VMEM((n_out * per + 1, width, edge), F32),
        ],
        compiler_params=pltpu.CompilerParams(vmem_limit_bytes=51 << 20),
        cost_estimate=pl.CostEstimate(
            flops=6 * slots * width * edge * edge, bytes_accessed=14 << 20, transcendentals=0
        ),
        name="spmm_back" if transposed else "spmm",
    )(table, *sources, values)


def stage_kernel(source, out):
    out[...] = source[...]


def stage(x):
    vmem = pl.BlockSpec(memory_space=pltpu.VMEM)
    return pl.pallas_call(
        stage_kernel,
        in_specs=[vmem],
        out_specs=vmem,
        out_shape=jax.ShapeDtypeStruct(x.shape, x.dtype),
        compiler_params=pltpu.CompilerParams(vmem_limit_bytes=4 << 20),
        cost_estimate=pl.CostEstimate(flops=0, bytes_accessed=1 << 18, transcendentals=0),
        name="stage",
    )(x)


def mid_kernel(n_rep, scale, place, *refs):
    aggs = refs[:n_rep]
    cots = refs[n_rep : 2 * n_rep]
    weight, weight_t, out, mixed_grad, sent = refs[2 * n_rep : 2 * n_rep + 5]
    agg, cot, act = refs[2 * n_rep + 5 :]
    quarter = aggs[0].shape[0]
    me = place[0]
    for k in range(n_rep):
        at = pl.ds(pl.multiple_of((me ^ k) * quarter, quarter), quarter)
        agg[at, :] = aggs[k][...]
        cot[at, :] = cots[k][...]
    pre = dot3(weight_t[...], agg[...], NN)
    square = pre * pre
    curve = jnp.tanh(ROOT_2_PI * (pre + CUBIC * (square * pre)))
    half = 0.5 * (1.0 + curve)
    act[...] = pre * half
    slope = half + 0.5 * pre * (1.0 - curve * curve) * (
        ROOT_2_PI * (1.0 + 3.0 * CUBIC * square)
    )
    grad = cot[...] * slope
    own = pl.ds(pl.multiple_of(me * quarter, quarter), quarter)
    mine = dot3(weight[own, :], grad, NN)
    length = mine.shape[1]
    mixed_grad[...] = mine
    sent[:, :length] = mine
    sent[:, length:] = dot3(agg[own, :], grad, NT) * scale
    out[...] = act[own, :]


def mid(place, aggs, cots, weight, weight_t, scale):
    n_rep = len(aggs)
    quarter, length = aggs[0].shape
    width = weight.shape[0]
    vmem = pl.BlockSpec(memory_space=pltpu.VMEM)
    return pl.pallas_call(
        functools.partial(mid_kernel, n_rep, scale),
        in_specs=[pl.BlockSpec(memory_space=pltpu.SMEM)] + [vmem] * (2 * n_rep + 2),
        out_specs=[vmem] * 3,
        out_shape=[
            jax.ShapeDtypeStruct((quarter, length), F32),
            jax.ShapeDtypeStruct((quarter, length), F32),
            jax.ShapeDtypeStruct((quarter, length + width), F32),
        ],
        scratch_shapes=[pltpu.VMEM((width, length), F32)] * 3,
        compiler_params=pltpu.CompilerParams(vmem_limit_bytes=16 << 20),
        cost_estimate=pl.CostEstimate(
            flops=8 * width * width * length, bytes_accessed=4 << 20, transcendentals=0
        ),
        name="mid",
    )(place, *aggs, *cots, weight, weight_t)


def join_kernel(mine, got, grad, grad_got, out):
    length = mine.shape[1]
    out[:, :length] = mine[...] + got[...]
    out[:, length:] = grad[...] + grad_got[...]


def total_kernel(n, mine, got, grad, grad_got, *refs):
    length = mine.shape[1]
    joined, (out, weight_out) = refs[:n], refs[n:]
    total = mine[...] + got[...]
    weight_total = grad[...] + grad_got[...]
    for ref in joined:
        total = total + ref[:, :length]
        weight_total = weight_total + ref[:, length:]
    out[...] = total
    weight_out[...] = weight_total


def small(body, shapes, *args):
    vmem = pl.BlockSpec(memory_space=pltpu.VMEM)
    return pl.pallas_call(
        body,
        in_specs=[vmem] * len(args),
        out_specs=[vmem] * len(shapes),
        out_shape=[jax.ShapeDtypeStruct(shape, F32) for shape in shapes],
        compiler_params=pltpu.CompilerParams(vmem_limit_bytes=8 << 20),
        cost_estimate=pl.CostEstimate(flops=0, bytes_accessed=1 << 19, transcendentals=0),
    )(*args)


def shift(x, axis, by):
    n = lax.axis_size(axis)
    return lax.ppermute(x, axis, [(i, (i + by) % n) for i in range(n)])


def swap(x, axis, bit):
    n = lax.axis_size(axis)
    return lax.ppermute(x, axis, [(i, i ^ bit) for i in range(n)])


def layer(features, weight, cotangent, tile_values, tile_row, tile_col, tile_kind, tile_count):
    n_row, n_col, n_rep = (lax.axis_size(a) for a in ("row", "col", "rep"))
    row, col, rep = (lax.axis_index(a) for a in ("row", "col", "rep"))
    stretch = features.shape[1]
    per = stretch // tile_values.shape[1]
    slots = tile_kind.shape[0]

    def relative(tile, at, n):
        stretch_of = tile // per
        far = (stretch_of // 2 - at // 2) % (n // 2)
        return (far * 2 + ((stretch_of ^ at) & 1)) * per + tile % per

    by_row = relative(tile_row, col, n_col)
    by_col = relative(tile_col, row, n_row)
    ids = jnp.arange(slots, dtype=jnp.int32)
    packed = (tile_kind << 2 * BITS) + (by_row << BITS) + by_col
    key = jnp.where(ids < tile_count[0], tile_kind, slots) * slots + ids
    rank = jnp.sum((key[None, :] < key[:, None]).astype(jnp.int32), axis=1)
    ordered = jnp.sum(jnp.where(rank[None, :] == ids[:, None], packed[None, :], 0), axis=1)
    table = jnp.concatenate([ordered, tile_count])
    blocks = []
    for k in range(n_row // 2):
        mine = shift(features, "row", -2 * k) if k else features
        blocks += [mine, swap(mine, "row", 1)]
    blocks[0] = stage(features)
    cots = [cotangent]
    for k in range(1, n_rep):
        cots.append(swap(cotangent, "rep", k))
    parts = spmm(table, blocks, tile_values, n_col, False)
    sums = [None, None]
    for z in (1, 0):
        total = parts[z]
        for k in range(1, n_col // 2):
            got = shift(parts[2 * k + z], "col", 2 * k)
            total = total + got
        sums[z] = total
    far = swap(sums[1], "col", 1)
    agg = sums[0] + far
    aggs = [agg]
    for k in range(1, n_rep):
        aggs.append(swap(agg, "rep", k))
    place = rep.astype(jnp.int32)[None]
    node_total = stretch * n_row * n_col
    output, mixed_grad, sent = mid(
        place, aggs, cots, weight, weight.T, float(node_total) ** (-0.5)
    )
    far = swap(mixed_grad, "col", 1)
    blocks = [mixed_grad, far]
    weight_grad = sent[:, stretch:]
    for k in range(1, n_col // 2):
        got = shift(sent, "col", -2 * k)
        weight_grad = weight_grad + got[:, stretch:]
        blocks += [got, shift(far, "col", -2 * k)]

    def add_swapped(x, axis, bit):
        return x + swap(x, axis, bit)

    weight_grad = add_swapped(weight_grad, "col", 1)
    parts = spmm(table, blocks, tile_values, n_row, True)
    grad_got = swap(weight_grad, "row", 1)
    near = None
    joined = []
    for k in (2, 1, 3, 0):
        got = swap(parts[2 * k + 1], "row", 1)
        near = (parts[2 * k], got, weight_grad, grad_got)
        if k:
            shape = (got.shape[0], got.shape[1] + weight_grad.shape[1])
            (total,) = small(join_kernel, [shape], *near)
            joined.append(shift(total, "row", 2 * k))
    input_grad, weight_grad = small(
        functools.partial(total_kernel, len(joined)),
        [features.shape, weight_grad.shape],
        *near,
        *joined,
    )
    return (output, input_grad, weight_grad)


def solution(mesh):
    return jax.shard_map(
        layer,
        mesh=mesh,
        in_specs=(
            P("rep", ("col", "row")),
            P(),
            P("rep", ("row", "col")),
            P(("row", "col"), None, None),
            P(("row", "col")),
            P(("row", "col")),
            P(("row", "col")),
            P(("row", "col")),
        ),
        out_specs=(P("rep", ("row", "col")), P("rep", ("col", "row")), P("rep", None)),
        check_vma=False,
    )
```
